512 devices in a mesh: ctx: 16 (over x_lo, y, core), dp: 32 (over x_hi, z).
Axes of the slice: x: 4 (x_hi: 2, x_lo: 2; x = x_hi * 2 + x_lo), y: 4, z: 16, core: 2. Of those that a mesh axis runs over, the one named last changes fastest.
Arguments:
- token_ids: int32 [32, 2048], P('dp', 'ctx'), may hold values from 0 to 511
- feature_table: bfloat16 [3072, 512], replicated, may hold values from -6 to 6
- short_weight: float32 [3072, 7], replicated, may hold values from -3 to 3
- residue: float32 [1024, 16], replicated, may hold values from -0.09375 to 0.09375
- rates: float32 [16], replicated, may hold values from 0.3 to 64
- skip_gain: float32 [1024], replicated, may hold values from 0.5 to 1.5
- grad_out: bfloat16 [32, 1024, 2048], P('dp', None, 'ctx'), may hold values from -0.0029296875 to 0.0029296875
Outputs:
- mixed: bfloat16 [32, 1024, 2048], P('dp', None, 'ctx')
- grad_residue: float32 [1024, 16], replicated
- grad_rate: float32 [16], replicated
The draws below stay inside these ranges and needn't reach their ends.
All inputs are finite; a program needn't handle non-finite values.
Results may differ from the reference program's by a relative error of at most 0.0065.
Values may be sent and summed in bfloat16 or wider, within the bound.
A program may use at most 64 MiB of HBM per device.

```python
import math
import jax
import jax.numpy as jnp
from jax import lax

CH = 1024
VOCAB = 512
MODES = 16
SHORT = 7
FEAT = 3072
SEQ = 2048
SEQS = 32


def plant(values, stream_key, least, largest):
    longest = values.shape.index(max(values.shape))
    spots = []
    for shift in (0, 1):
        where = [jax.random.randint(jax.random.fold_in(stream_key, axis), (), 0, length) for axis, length in enumerate(values.shape)]
        where[longest] = (where[longest] + shift) % values.shape[longest]
        spots.append(tuple(where))
    return values.at[spots[0]].set(least).at[spots[1]].set(largest)


def block_scale(own_key, dims, cuts, smallest, top_value):
    def one(axis_at, blocks):
        draws = jax.random.uniform(jax.random.fold_in(jax.random.fold_in(own_key, 6), axis_at), (blocks,), jnp.float32, smallest / len(cuts), top_value / len(cuts))
        return jnp.repeat(jnp.exp(draws), dims[axis_at] // blocks).reshape((-1,) + (1,) * (len(dims) - axis_at - 1))

    factor_of = one(*cuts[0])
    for cut in cuts[1:]:
        factor_of = factor_of * one(*cut)
    return factor_of


def gaussian(rng, shape, scale, limit, pieces=(), held_as=jnp.bfloat16):
    level = block_scale(rng, shape, pieces, -0.22, 0.18) if pieces else 1.0
    values = jax.random.normal(rng, shape, jnp.float32) * scale * level
    return jnp.minimum(jnp.maximum(values, -limit), limit).astype(held_as)


def setup_inputs(seed: int = 0) -> dict:
    keys = jax.random.split(jax.random.key(seed), 8)
    return {
        "token_ids": plant(jax.random.randint(keys[0], (SEQS, SEQ), 0, VOCAB), jax.random.fold_in(keys[0], 1), 0, VOCAB - 1).astype(jnp.int32),
        "feature_table": gaussian(keys[1], (FEAT, VOCAB), 1.0, 6.0),
        "short_weight": gaussian(keys[2], (FEAT, SHORT), 0.5, 3.0, (), jnp.float32),
        "residue": gaussian(keys[3], (CH, MODES), (MODES * SEQ // 8) ** -0.5, 0.09375, (), jnp.float32),
        "rates": jnp.clip(jnp.exp(jax.random.uniform(keys[4], (MODES,), jnp.float32, math.log(0.3), math.log(64.0))), 0.3, 64.0),
        "skip_gain": jnp.clip(1.0 + 0.1 * jax.random.normal(keys[5], (CH,), jnp.float32), 0.5, 1.5),
        "grad_out": gaussian(keys[6], (SEQS, CH, SEQ), (1.0 / (8 * (SEQS * SEQ) ** 0.5)), 0.0029296875, ((0, 32), (2, 16))),
    }


def reference(token_ids, feature_table, short_weight, residue, rates, skip_gain, grad_out):
    steps_i = jnp.arange(SEQ, dtype=jnp.int32)
    steps_f = steps_i.astype(jnp.float32)
    period = 2 * MODES + 2
    mode_number = jnp.arange(MODES, dtype=jnp.int32)[:, None] + 1
    angles = (mode_number * steps_i[None, :] % period).astype(jnp.float32) * (2.0 * math.pi / period)
    oscillation = jnp.cos(angles)

    def make_taps(weights, decays):
        powers = jnp.exp(-decays[:, None] * steps_f[None, :] / SEQ) * oscillation
        return jnp.dot(weights, powers, precision=lax.Precision.HIGHEST)

    def circular_conv(filt, signal):
        spectrum = jnp.fft.rfft(signal, SEQ) * jnp.fft.rfft(filt, SEQ)
        return jnp.fft.irfft(spectrum, SEQ)

    def one_sequence(pair):
        ids_row, cotangent = pair
        features = jnp.take(feature_table, ids_row, axis=1).astype(jnp.float32)
        padded = jnp.concatenate([features[:, SEQ - (SHORT - 1):], features], axis=1)
        mixer = jnp.zeros((FEAT, SEQ), jnp.float32)
        for offset in range(SHORT):
            mixer = mixer + short_weight[:, offset:offset + 1] * padded[:, offset:offset + SEQ]
        queries = mixer[:CH]
        keys_part = mixer[CH:2 * CH]
        values_part = mixer[2 * CH:]
        gated = lax.optimization_barrier((keys_part * values_part).astype(jnp.bfloat16)).astype(jnp.float32)
        conv, pullback = jax.vjp(lambda weights, decays: circular_conv(make_taps(weights, decays), gated), residue, rates)
        mixed = (queries * (conv + skip_gain[:, None] * gated)).astype(jnp.bfloat16)
        dconv = queries * cotangent.astype(jnp.float32)
        grad_weights, grad_decays = pullback(dconv)
        return (mixed, grad_weights, grad_decays)
    mixed, grad_weights, grad_decays = lax.map(one_sequence, (token_ids, grad_out))
    return (mixed, lax.optimization_barrier(jnp.sum(grad_weights, axis=0)), lax.optimization_barrier(jnp.sum(grad_decays, axis=0)))
```

```python
import functools
import math

import jax
import jax.numpy as jnp
from jax import lax
from jax.experimental import pallas as pl
from jax.experimental.pallas import tpu as pltpu
from jax.sharding import PartitionSpec as P

MESH = pl.DeviceIdType.MESH
F32 = jnp.float32
BF16 = jnp.bfloat16
TILE = 256
HALF = 8
LANES = 128


def filter_tables(rates, block, seq_len):
    modes = rates.shape[0]
    period = 2 * modes + 2
    number = jnp.arange(modes, dtype=jnp.int32)[:, None] + 1

    def angle(steps):
        return (number * steps[None, :] % period).astype(F32) * (2.0 * math.pi / period)

    def decay(steps):
        return jnp.exp(-rates[:, None] * steps.astype(F32)[None, :] / seq_len)

    pos = jnp.arange(block, dtype=jnp.int32)
    rise = jnp.exp(rates[:, None] * pos.astype(F32)[None, :] / seq_len)
    cos_p, sin_p = jnp.cos(angle(pos)), jnp.sin(angle(pos))
    wrap = pos + seq_len
    near, far = decay(pos), decay(wrap)
    near_c, near_s = near * cos_p, near * sin_p
    far_c, far_s = far * jnp.cos(angle(wrap)), far * jnp.sin(angle(wrap))
    src_c, src_s = rise * cos_p, rise * sin_p
    causal = pos[:, None] >= pos[None, :]
    out_c = jnp.where(causal[None], near_c[:, :, None], far_c[:, :, None])
    out_s = jnp.where(causal[None], near_s[:, :, None], far_s[:, :, None])
    power = out_c * src_c[:, None, :] + out_s * src_s[:, None, :]
    gap = pos[:, None] - pos[None, :]
    delay = jnp.where(causal, gap, gap + seq_len).astype(F32) / seq_len
    slope = -power * delay[None]
    dense = jnp.stack([power, slope], axis=1).reshape(2 * modes * block, block).astype(BF16)

    def state(steps):
        real = decay(steps) * jnp.cos(angle(steps))
        imag = decay(steps) * jnp.sin(angle(steps))
        weight = (steps.astype(F32) / seq_len)[None, :]
        rows = jnp.stack([real, imag, real * weight, imag * weight], axis=0)
        rows = rows.reshape(4, modes // HALF, HALF, block).transpose(1, 0, 2, 3)
        return rows.reshape(4 * modes, block).astype(BF16), real, imag

    into, _, _ = state(block - 1 - pos)
    onto, real, imag = state(pos + 1)
    spread = jnp.stack([real, -imag], axis=0).reshape(2, modes // HALF, HALF, block)
    spread = spread.transpose(3, 1, 0, 2).reshape(block, 2 * modes).astype(BF16)
    return dense, into, onto, spread


def local_kernel(ids_ref, table_ref, short_ref, dense_ref, into_ref, onto_ref, res_ref, skip_ref,
                 gout_ref, query_ref, base_ref, msg_ref, feat, sums):
    rows = ids_ref.shape[0]
    block = dense_ref.shape[1]
    modes = res_ref.shape[0]
    vocab = table_ref.shape[2]
    columns = lax.broadcasted_iota(jnp.int32, (rows, vocab), 1)
    onehot = jnp.where(columns == ids_ref[...], 1.0, 0.0).astype(BF16)
    mixed = []
    for part in range(3):
        feat[part] = lax.dot_general(
            onehot, table_ref[part], (((1,), (1,)), ((), ())), preferred_element_type=F32
        )
        total = short_ref[part, 0:1, :] * feat[part, 2 : 2 + block, :]
        for tap in range(1, 7):
            total = total + short_ref[part, tap : tap + 1, :] * feat[part, 2 + tap : 2 + tap + block, :]
        mixed.append(total)
    query = mixed[0]
    gated = (mixed[1] * mixed[2]).astype(BF16)
    query_ref[...] = query
    dconv = query * gout_ref[...].astype(F32).T
    base = skip_ref[...] * gated.astype(F32)
    for mode in range(modes):
        for kind in range(2):
            row = (2 * mode + kind) * block
            term = jnp.dot(dense_ref[row : row + block, :], gated, preferred_element_type=F32)
            if kind == 0:
                base = base + res_ref[mode : mode + 1, :] * term
            slot = (mode // HALF) * 2 * HALF + kind * HALF + mode % HALF
            sums[slot : slot + 1, :] = jnp.sum(dconv * term, axis=0, keepdims=True)
    base_ref[...] = base
    upper = jnp.dot(into_ref[...], gated, preferred_element_type=F32).astype(BF16)
    lower = jnp.dot(onto_ref[...], dconv.astype(BF16), preferred_element_type=F32).astype(BF16)
    totals = sums[...].astype(BF16)
    for group in range(TILE // LANES):
        lane = slice(group * LANES, (group + 1) * LANES)
        for half in range(2):
            slot = group * 2 + half
            msg_ref[slot, 0:32, :] = upper[half * 32 : half * 32 + 32, lane]
            msg_ref[slot, 32:64, :] = lower[half * 32 : half * 32 + 32, lane]
            msg_ref[slot, 64:80, :] = totals[half * 16 : half * 16 + 16, lane]


def exchange_kernel(ctx_n, dp_n, rows_n, msg_ref, turn_ref, res_ref, state_ref, grad_ref,
                    got, backs, terms, parts, column, sem_a, sem_b, sem_c, sem_d, sem_e,
                    rsem_a, rsem_b, rsem_c, rsem_d, rsem_e, local_sem):
    me = lax.axis_index("ctx")
    rank = lax.axis_index("dp")
    low = lax.rem(rank, rows_n)
    base = rank - low

    barrier = pltpu.get_barrier_semaphore()

    def greet_ctx(step, carry):
        pl.semaphore_signal(barrier, inc=1, device_id={"ctx": lax.rem(me + step, ctx_n)}, device_id_type=MESH)
        return carry

    def greet_dp(step, carry):
        pl.semaphore_signal(barrier, inc=1, device_id={"dp": lax.rem(rank + step, dp_n)}, device_id_type=MESH)
        return carry

    lax.fori_loop(1, ctx_n, greet_ctx, 0)
    lax.fori_loop(1, dp_n, greet_dp, 0)
    pl.semaphore_wait(barrier, ctx_n - 1 + dp_n - 1)

    def run(count, make):
        def body(step, carry):
            make(step).start()
            return carry
        lax.fori_loop(1, count, body, 0)

    def land(count, make):
        def body(step, carry):
            make(step).wait_recv()
            return carry
        lax.fori_loop(1, count, body, 0)

    def left(count, make):
        def body(step, carry):
            make(step).wait_send()
            return carry
        lax.fori_loop(1, count, body, 0)

    def over_ctx(source, target, send, recv):
        def make(step, arriving):
            peer = lax.rem(me + step, ctx_n)
            slot = lax.rem(me + ctx_n - step, ctx_n) if arriving else me
            return pltpu.make_async_remote_copy(
                src_ref=source(peer), dst_ref=target.at[slot], send_sem=send.at[step],
                recv_sem=recv.at[slot], device_id={"ctx": peer}, device_id_type=MESH)
        return (lambda step: make(step, False)), (lambda step: make(step, True))

    out_a, in_a = over_ctx(lambda peer: msg_ref.at[peer], got, sem_a, rsem_a)
    run(ctx_n, out_a)
    own = pltpu.make_async_copy(msg_ref.at[me], got.at[me], local_sem.at[0])
    own.start()
    own.wait()
    land(ctx_n, in_a)

    turn_c, turn_s, last_c, last_s = (turn_ref[i] for i in range(4))

    def states(index, first):
        pair = got[index, first : first + 16, :].astype(F32)
        return pair[:HALF], pair[HALF:]

    step_len = 1.0 / ctx_n

    def times_turn(real, imag):
        return real * turn_c - imag * turn_s, real * turn_s + imag * turn_c

    def times_last(real, imag):
        return real * last_c - imag * last_s, real * last_s + imag * last_c

    zero = jnp.zeros((HALF, LANES), F32)

    def advance(carry, index):
        hr, hi, dr, di = carry
        ur, ui = states(index, 0)
        wr, wi = states(index, 16)
        nr, ni = times_turn(hr, hi)
        er, ei = times_turn(dr + step_len * hr, di + step_len * hi)
        return nr + ur, ni + ui, er + wr, ei + wi

    def warm(index, carry):
        return advance(carry, index)

    start = lax.fori_loop(1, ctx_n, warm, (zero, zero, zero, zero))
    span = step_len * (ctx_n - 2)

    def visit(index, carry):
        hr, hi, dr, di, gsum, dsum = carry
        backs[index, 0:16, :] = jnp.concatenate([hr, hi], axis=0).astype(BF16)
        vr, vi = states(index, 32)
        xr, xi = states(index, 48)
        g0, d0 = states(index, 64)
        gsum = gsum + (g0 + (vr * hr - vi * hi))
        dsum = dsum + (d0 - ((xr * hr - xi * hi) + (vr * dr - vi * di)))
        old = lax.rem(index + 1, ctx_n)
        ur, ui = states(old, 0)
        wr, wi = states(old, 16)
        lr, li = times_last(ur, ui)
        pr, pi_ = times_last(wr + span * ur, wi + span * ui)
        hr, hi, dr, di = advance((hr - lr, hi - li, dr - pr, di - pi_), index)
        return hr, hi, dr, di, gsum, dsum

    final = lax.fori_loop(0, ctx_n, visit, start + (zero, zero))
    gsum = final[4]
    dsum = final[5] * res_ref[...]

    out_b, in_b = over_ctx(lambda peer: backs.at[peer], state_ref, sem_b, rsem_b)
    for row in range(HALF):
        terms[row] = gsum[row : row + 1, :]
        terms[HALF + row] = dsum[row : row + 1, :]

    def over_dp(arriving):
        def make(step):
            peer = lax.rem(rank + step, dp_n)
            slot = lax.rem(rank + dp_n - step, dp_n) if arriving else rank
            return pltpu.make_async_remote_copy(
                src_ref=terms.at[lax.rem(peer, rows_n)], dst_ref=parts.at[slot], send_sem=sem_c.at[step],
                recv_sem=rsem_c.at[slot], device_id={"dp": peer}, device_id_type=MESH)
        return make

    run(dp_n, over_dp(False))
    keep = pltpu.make_async_copy(terms.at[low], parts.at[rank], local_sem.at[1])
    keep.start()
    run(ctx_n, out_b)
    mine = pltpu.make_async_copy(backs.at[me], state_ref.at[me], local_sem.at[2])
    mine.start()
    keep.wait()
    land(dp_n, over_dp(True))
    column[...] = jnp.sum(parts[...], axis=0)

    def over_rows(arriving):
        def make(step):
            other = lax.rem(low + step, rows_n)
            slot = lax.rem(low + rows_n - step, rows_n) if arriving else low
            return pltpu.make_async_remote_copy(
                src_ref=column, dst_ref=grad_ref.at[me, slot], send_sem=sem_d.at[step],
                recv_sem=rsem_d.at[slot], device_id={"dp": base + other}, device_id_type=MESH)
        return make

    run(rows_n, over_rows(False))
    place = pltpu.make_async_copy(column, grad_ref.at[me, low], local_sem.at[3])
    place.start()
    place.wait()
    land(rows_n, over_rows(True))
    out_e, in_e = over_ctx(lambda peer: grad_ref.at[me], grad_ref, sem_e, rsem_e)
    run(ctx_n, out_e)
    mine.wait()
    land(ctx_n, in_b)
    land(ctx_n, in_e)
    left(ctx_n, out_a)
    left(ctx_n, out_b)
    left(dp_n, over_dp(False))
    left(rows_n, over_rows(False))
    left(ctx_n, out_e)


def finish_kernel(state_ref, res_ref, spread_ref, query_ref, base_ref, out_ref):
    columns = []
    for group in range(TILE // LANES):
        columns.append(jnp.concatenate(
            [state_ref[group * 2].astype(F32), state_ref[group * 2 + 1].astype(F32)], axis=0))
    state = (jnp.concatenate(columns, axis=1) * res_ref[...]).astype(BF16)
    conv = jnp.dot(spread_ref[...], state, preferred_element_type=F32)
    out_ref[...] = (query_ref[...] * (base_ref[...] + conv)).T.astype(BF16)


def per_device(dp_n, token_ids, feature_table, short_weight, residue, rates, skip_gain, grad_out):
    block = token_ids.shape[1]
    ctx_n = lax.axis_size("ctx")
    seq_len = block * ctx_n
    channels, modes = residue.shape
    vocab = feature_table.shape[1]
    taps = short_weight.shape[1]
    rows_n = 2 * HALF
    me = lax.axis_index("ctx")

    ids = token_ids[0]
    route = [((i - 1) % ctx_n, i) for i in range(ctx_n)]
    previous = lax.ppermute(ids[block - (taps - 1) :], "ctx", route)
    ids_col = jnp.concatenate([jnp.full((2,), -1, jnp.int32), previous, ids])[:, None]
    rows = ids_col.shape[0]

    dense, into, onto, spread = filter_tables(rates, block, seq_len)
    short = jnp.pad(short_weight.T, ((0, 1), (0, 0))).reshape(8, 3, channels).transpose(1, 0, 2)
    table = feature_table.reshape(3, channels, vocab)
    res_t = residue.T
    whole = lambda shape: pl.BlockSpec(shape, lambda i: (0,) * len(shape))
    lanes = lambda n: pl.BlockSpec((n, TILE), lambda i: (0, i))

    query, base, msg = pl.pallas_call(
        local_kernel,
        grid=(channels // TILE,),
        in_specs=[
            whole((rows, 1)),
            pl.BlockSpec((3, TILE, vocab), lambda i: (0, i, 0)),
            pl.BlockSpec((3, 8, TILE), lambda i: (0, 0, i)),
            whole(dense.shape), whole(into.shape), whole(onto.shape),
            lanes(modes), lanes(1),
            pl.BlockSpec((TILE, block), lambda i: (i, 0)),
        ],
        out_specs=[lanes(block), lanes(block),
                   pl.BlockSpec((2 * TILE // LANES, 80, LANES), lambda i: (i, 0, 0))],
        out_shape=[jax.ShapeDtypeStruct((block, channels), F32),
                   jax.ShapeDtypeStruct((block, channels), F32),
                   jax.ShapeDtypeStruct((ctx_n, 80, LANES), BF16)],
        scratch_shapes=[pltpu.VMEM((3, rows, TILE), F32), pltpu.VMEM((2 * modes, TILE), F32)],
        compiler_params=pltpu.CompilerParams(vmem_limit_bytes=40 * 1024 * 1024),
    )(ids_col, table, short, dense, into, onto, res_t, skip_gain[None, :], grad_out[0])

    half, group = me % 2, me // 2
    own_rates = lax.dynamic_slice(rates, (half * HALF,), (HALF,))
    own_mode = half * HALF + 1 + jnp.arange(HALF, dtype=jnp.int32)
    period = 2 * modes + 2

    def turn(steps):
        angle = (own_mode * steps % period).astype(F32) * (2.0 * math.pi / period)
        size = jnp.exp(-own_rates * (steps / seq_len))
        return [size * jnp.cos(angle), size * jnp.sin(angle)]

    turns = jnp.stack(turn(block) + turn(block * (ctx_n - 2)))
    turns = jnp.broadcast_to(turns[:, :, None], (4, HALF, LANES))
    own_res = lax.dynamic_slice(res_t, (half * HALF, group * LANES), (HALF, LANES))

    dma = pltpu.SemaphoreType.DMA
    vmem = pl.BlockSpec(memory_space=pltpu.VMEM)
    states, grads = pl.pallas_call(
        functools.partial(exchange_kernel, ctx_n, dp_n, rows_n),
        in_specs=[vmem] * 3,
        out_specs=[vmem] * 2,
        out_shape=[jax.ShapeDtypeStruct((ctx_n, 16, LANES), BF16),
                   jax.ShapeDtypeStruct((ctx_n, rows_n, 1, LANES), F32)],
        scratch_shapes=[
            pltpu.VMEM((ctx_n, 80, LANES), BF16),
            pltpu.VMEM((ctx_n, 16, LANES), BF16),
            pltpu.VMEM((rows_n, 1, LANES), F32),
            pltpu.VMEM((dp_n, 1, LANES), F32),
            pltpu.VMEM((1, LANES), F32),
            dma((ctx_n,)), dma((ctx_n,)), dma((dp_n,)), dma((rows_n,)), dma((ctx_n,)),
            dma((ctx_n,)), dma((ctx_n,)), dma((dp_n,)), dma((rows_n,)), dma((ctx_n,)),
            dma((4,)),
        ],
        compiler_params=pltpu.CompilerParams(collective_id=0, has_side_effects=True),
    )(msg, turns, own_res)

    res_rows = jnp.concatenate([res_t[:HALF], res_t[:HALF], res_t[HALF:], res_t[HALF:]], axis=0)
    mixed = pl.pallas_call(
        finish_kernel,
        grid=(channels // TILE,),
        in_specs=[
            pl.BlockSpec((2 * TILE // LANES, 16, LANES), lambda i: (i, 0, 0)),
            lanes(2 * modes), whole((block, 2 * modes)), lanes(block), lanes(block),
        ],
        out_specs=pl.BlockSpec((TILE, block), lambda i: (i, 0)),
        out_shape=jax.ShapeDtypeStruct((channels, block), BF16),
    )(states, res_rows, spread, query, base)

    parts = grads.reshape(ctx_n // 2, 2, 2, HALF, LANES)
    grad_residue = parts[:, :, 0].transpose(0, 3, 1, 2).reshape(channels, modes)
    grad_rate = jnp.sum(parts[:, :, 1], axis=(0, 3)).reshape(modes)
    return (mixed[None], grad_residue, grad_rate)


def solution(mesh):
    return jax.shard_map(
        functools.partial(per_device, mesh.shape["dp"]),
        mesh=mesh,
        in_specs=(P("dp", "ctx"), P(), P(), P(), P(), P(), P("dp", None, "ctx")),
        out_specs=(P("dp", None, "ctx"), P(), P()),
        check_vma=False,
    )
```

```python
import functools
import math

import jax
import jax.numpy as jnp
from jax import lax
from jax.experimental import pallas as pl
from jax.experimental.pallas import tpu as pltpu
from jax.sharding import PartitionSpec as P

MESH = pl.DeviceIdType.MESH
F32 = jnp.float32
BF16 = jnp.bfloat16
TILE = 256
HALF = 8
LANES = 128


def ids_kernel(ctx_n, ids_ref, prev_ref, send_sem, recv_sem):
    me = lax.axis_index("ctx")
    right, left = lax.rem(me + 1, ctx_n), lax.rem(me + ctx_n - 1, ctx_n)
    barrier = pltpu.get_barrier_semaphore()
    pl.semaphore_signal(barrier, inc=1, device_id={"ctx": left}, device_id_type=MESH)
    pl.semaphore_wait(barrier, 1)
    copy = pltpu.make_async_remote_copy(
        src_ref=ids_ref, dst_ref=prev_ref, send_sem=send_sem, recv_sem=recv_sem,
        device_id={"ctx": right}, device_id_type=MESH)
    copy.start()
    copy.wait()


def layer_kernel(ctx_n, dp_n, rates_ref, ids_hbm, prev_hbm, short_hbm, res_hbm, skip_hbm, table_hbm, gout_hbm,
                 out_hbm, gres_ref, grate_ref,
                 ids_ref, prev_ref, short_ref, res_ref, skip_ref, out_ref, gated_s, dconv_s, late, got_late,
                 table, gout, dense, into, onto, spread, rate_rows, feat, sums, query_s, base_s,
                 msg, got, backs, state, parts, grads,
                 sem_a, sem_b, sem_c, sem_e, sem_f, rsem_a, rsem_b, rsem_c, rsem_e, rsem_f, local_sem):
    me = lax.axis_index("ctx")
    rank = lax.axis_index("dp")
    modes, channels = res_ref.shape
    block = out_ref.shape[1]
    vocab = table.shape[2]
    taps = short_ref.shape[0]
    seq_len = block * ctx_n
    tiles = channels // TILE
    period = 2 * modes + 2

    barrier = pltpu.get_barrier_semaphore()

    def greet_dp(step, carry):
        pl.semaphore_signal(barrier, inc=1, device_id={"dp": lax.rem(rank + step, dp_n)}, device_id_type=MESH)
        return carry

    def greet_ctx(step, carry):
        pl.semaphore_signal(barrier, inc=1, device_id={"ctx": lax.rem(me + step, ctx_n)}, device_id_type=MESH)
        return carry

    lax.fori_loop(1, dp_n, greet_dp, 0)
    lax.fori_loop(1, ctx_n, greet_ctx, 0)

    small = []
    pairs = ((ids_hbm, ids_ref), (prev_hbm, prev_ref), (short_hbm, short_ref), (res_hbm, res_ref),
             (skip_hbm, skip_ref), (gout_hbm, gout))
    for index, (source, target) in enumerate(pairs):
        small.append(pltpu.make_async_copy(source, target, local_sem.at[tiles + index]))
        small[-1].start()
    loads = []
    for tile in range(tiles):
        part = pl.ds(tile * TILE, TILE)
        loads.append(pltpu.make_async_copy(table_hbm.at[:, part], table.at[:, part], local_sem.at[tile]))
        loads[-1].start()

    def wave_angle(product):
        turns = jnp.floor(product * (1.0 / period))
        return (product - period * turns) * (2.0 * math.pi / period)

    for mode in range(modes):
        rate_rows[mode : mode + 1, :] = jnp.full((1, LANES), rates_ref[mode], F32)
    decay_rows = rate_rows[...] * (-1.0 / seq_len)
    number = lax.broadcasted_iota(jnp.int32, (modes, block), 0).astype(F32) + 1.0
    lane = lax.broadcasted_iota(jnp.int32, (modes, block), 1).astype(F32)

    def fill(ref, steps):
        size = jnp.exp(decay_rows * steps)
        angle = wave_angle(number * steps)
        real, imag = size * jnp.cos(angle), size * jnp.sin(angle)
        weight = steps * (1.0 / seq_len)
        for index, value in enumerate((real, imag, real * weight, imag * weight)):
            for half in range(2):
                ref[half * 32 + index * HALF : half * 32 + (index + 1) * HALF, :] = value[half * HALF : (half + 1) * HALF]
        return real, imag

    fill(into, (block - 1.0) - lane)
    real, imag = fill(onto, lane + 1.0)
    spread[...] = jnp.concatenate(
        [real[:HALF], -imag[:HALF], real[HALF:], -imag[HALF:], jnp.zeros((block - 2 * modes, block), F32)],
        axis=0).T.astype(BF16)

    gap = (lax.broadcasted_iota(jnp.int32, (block, block), 0)
           - lax.broadcasted_iota(jnp.int32, (block, block), 1)).astype(F32)
    delay = jnp.where(gap < 0.0, gap + seq_len, gap)
    base_wave = jnp.cos(wave_angle(delay))
    share = delay * (-1.0 / seq_len)

    def fill_dense(mode, carry):
        before, now = carry
        power = jnp.exp(share * rates_ref[mode]) * now
        row = pl.multiple_of(mode * 2 * block, 2 * block)
        dense[pl.ds(row, block), :] = power.astype(BF16)
        dense[pl.ds(row + block, block), :] = (power * share).astype(BF16)
        return now, 2.0 * base_wave * now - before


    for copy in small:
        copy.wait()

    def spell(ref):
        square = jnp.broadcast_to(ref[...].astype(F32), (block, block)).T
        return jnp.concatenate([square] * (vocab // block), axis=1)

    symbols = jnp.concatenate([spell(prev_ref)[block - 8 :], spell(ids_ref)], axis=0)
    columns = lax.broadcasted_iota(jnp.int32, symbols.shape, 1).astype(F32)
    onehot = jnp.where(columns == symbols, 1.0, 0.0).astype(BF16)

    def halves(value):
        upper = value.astype(BF16)
        return upper, (value - upper.astype(F32)).astype(BF16)

    into_b = jnp.concatenate(halves(into[...]), axis=0)
    onto_b = jnp.concatenate(halves(onto[...]), axis=0)
    states_n = 4 * modes

    for tile in range(tiles):
        loads[tile].wait()
        at = tile * TILE
        cols = pl.ds(at, TILE)
        mixed = []
        for part in range(3):
            feat[part] = lax.dot_general(
                onehot, table[part, cols, :], (((1,), (1,)), ((), ())), preferred_element_type=F32)
            wide = pl.ds(part * channels + at, TILE)
            total = short_ref[0:1, wide] * feat[part, 2 : 2 + block, :]
            for tap in range(1, taps):
                total = total + short_ref[tap : tap + 1, wide] * feat[part, 2 + tap : 2 + tap + block, :]
            mixed.append(total)
        gated = (mixed[1] * mixed[2]).astype(BF16)
        dconv = mixed[0] * gout[cols, :].astype(F32).T
        query_s[:, cols] = mixed[0]
        gated_s[:, cols] = gated
        dconv_s[:, cols] = dconv
        upper = jnp.dot(into_b, gated, preferred_element_type=F32)
        upper = upper[:states_n] + upper[states_n:]
        dconv_u, dconv_l = halves(dconv)
        lower = jnp.dot(onto_b, dconv_u, preferred_element_type=F32)
        lower = lower[:states_n] + lower[states_n:]
        lower = lower + jnp.dot(onto_b[:states_n], dconv_l, preferred_element_type=F32)
        for group in range(TILE // LANES):
            cut = slice(group * LANES, (group + 1) * LANES)
            for half in range(2):
                slot = (TILE // LANES * tile + group) * 2 + half
                msg[slot, 0:32, :] = upper[half * 32 : half * 32 + 32, cut]
                msg[slot, 32:64, :] = lower[half * 32 : half * 32 + 32, cut]

    lax.fori_loop(0, modes, fill_dense, (jnp.ones((block, block), F32), base_wave))
    pl.semaphore_wait(barrier, ctx_n - 1 + dp_n - 1)

    def run(count, make):
        def body(step, carry):
            make(step).start()
            return carry
        lax.fori_loop(1, count, body, 0)

    def land(count, make):
        def body(step, carry):
            make(step).wait_recv()
            return carry
        lax.fori_loop(1, count, body, 0)

    def left(count, make):
        def body(step, carry):
            make(step).wait_send()
            return carry
        lax.fori_loop(1, count, body, 0)

    def over_ctx(source, target, send, recv):
        def make(step, arriving):
            peer = lax.rem(me + step, ctx_n)
            slot = lax.rem(me + ctx_n - step, ctx_n) if arriving else me
            return pltpu.make_async_remote_copy(
                src_ref=source(peer), dst_ref=target.at[slot], send_sem=send.at[step],
                recv_sem=recv.at[slot], device_id={"ctx": peer}, device_id_type=MESH)
        return (lambda step: make(step, False)), (lambda step: make(step, True))

    out_a, in_a = over_ctx(lambda peer: msg.at[peer], got, sem_a, rsem_a)
    run(ctx_n, out_a)
    own = pltpu.make_async_copy(msg.at[me], got.at[me], local_sem.at[0])
    own.start()

    for tile in range(tiles):
        cols = pl.ds(tile * TILE, TILE)
        gated, dconv = gated_s[:, cols], dconv_s[:, cols]
        base = skip_ref[:, cols] * gated.astype(F32)
        for mode in range(modes):
            for kind in range(2):
                row = (2 * mode + kind) * block
                term = jnp.dot(dense[row : row + block, :], gated, preferred_element_type=F32)
                if kind == 0:
                    base = base + res_ref[mode : mode + 1, cols] * term
                slot = (mode // HALF) * 2 * HALF + kind * HALF + mode % HALF
                sums[slot : slot + 1, :] = jnp.sum(dconv * term, axis=0, keepdims=True)
        base_s[:, cols] = base
        totals = sums[...].astype(BF16)
        for group in range(TILE // LANES):
            cut = slice(group * LANES, (group + 1) * LANES)
            for half in range(2):
                slot = (TILE // LANES * tile + group) * 2 + half
                late[slot] = totals[half * 16 : half * 16 + 16, cut]

    out_f, in_f = over_ctx(lambda peer: late.at[peer], got_late, sem_f, rsem_f)
    run(ctx_n, out_f)
    own_late = pltpu.make_async_copy(late.at[me], got_late.at[me], local_sem.at[2])
    own_late.start()

    own_half = lax.rem(me, 2)
    own_group = me // 2
    first = pl.multiple_of(own_half * HALF, HALF)
    own_decay = rate_rows[pl.ds(first, HALF), :] * (-1.0 / seq_len)
    own_res = res_ref[pl.ds(first, HALF), pl.ds(pl.multiple_of(own_group * LANES, LANES), LANES)]
    own_number = (lax.broadcasted_iota(jnp.int32, (HALF, LANES), 0) + (own_half * HALF + 1)).astype(F32)

    def turn(steps):
        size = jnp.exp(own_decay * steps)
        angle = wave_angle(own_number * steps)
        return size * jnp.cos(angle), size * jnp.sin(angle)

    turn_c, turn_s = turn(float(block))
    last_c, last_s = turn(float(block * (ctx_n - 2)))
    step_len = 1.0 / ctx_n
    span = step_len * (ctx_n - 2)
    zero = jnp.zeros((HALF, LANES), F32)

    def states(index, start):
        pair = got[index, start : start + 16, :]
        return pair[:HALF], pair[HALF:]

    def times_turn(real, imag):
        return real * turn_c - imag * turn_s, real * turn_s + imag * turn_c

    def times_last(real, imag):
        return real * last_c - imag * last_s, real * last_s + imag * last_c

    def advance(index, carry):
        hr, hi, dr, di = carry
        ur, ui = states(index, 0)
        wr, wi = states(index, 16)
        nr, ni = times_turn(hr, hi)
        er, ei = times_turn(dr + step_len * hr, di + step_len * hi)
        return nr + ur, ni + ui, er + wr, ei + wi

    own.wait()
    land(ctx_n, in_a)
    carry = (zero, zero, zero, zero)
    for index in range(1, ctx_n):
        carry = advance(index, carry)
    gsum, dsum = zero, zero
    for index in range(ctx_n):
        hr, hi, dr, di = carry
        backs[index] = jnp.concatenate([hr, hi], axis=0).astype(BF16)
        vr, vi = states(index, 32)
        xr, xi = states(index, 48)
        gsum = gsum + (vr * hr - vi * hi)
        dsum = dsum - ((xr * hr - xi * hi) + (vr * dr - vi * di))
        if index < ctx_n - 1:
            ur, ui = states(index + 1, 0)
            wr, wi = states(index + 1, 16)
            lr, li = times_last(ur, ui)
            pr, pi_ = times_last(wr + span * ur, wi + span * ui)
            carry = advance(index, (hr - lr, hi - li, dr - pr, di - pi_))

    out_b, in_b = over_ctx(lambda peer: backs.at[peer], state, sem_b, rsem_b)
    run(ctx_n, out_b)
    mine = pltpu.make_async_copy(backs.at[me], state.at[me], local_sem.at[1])
    mine.start()
    own_late.wait()
    land(ctx_n, in_f)
    for index in range(ctx_n):
        pair = got_late[index].astype(F32)
        gsum = gsum + pair[:HALF]
        dsum = dsum + pair[HALF:]
    rate = jnp.broadcast_to(jnp.sum(dsum * own_res, axis=1, keepdims=True), (HALF, LANES))
    rate_u, rate_l = halves(rate)
    left_half = lax.broadcasted_iota(jnp.int32, (HALF, LANES), 1) < LANES // 2
    rate = jnp.where(left_half, rate_u.astype(F32), rate_l.astype(F32))
    parts[rank] = jnp.concatenate([gsum, rate], axis=0).astype(BF16)

    def over_dp(arriving):
        def make(step):
            peer = lax.rem(rank + step, dp_n)
            slot = lax.rem(rank + dp_n - step, dp_n) if arriving else rank
            return pltpu.make_async_remote_copy(
                src_ref=parts.at[rank], dst_ref=parts.at[slot], send_sem=sem_c.at[step],
                recv_sem=rsem_c.at[slot], device_id={"dp": peer}, device_id_type=MESH)
        return make

    run(dp_n, over_dp(False))
    mine.wait()
    land(ctx_n, in_b)

    for tile in range(tiles):
        cols = pl.ds(tile * TILE, TILE)
        pieces = []
        for group in range(TILE // LANES):
            slot = (TILE // LANES * tile + group) * 2
            pieces.append(jnp.concatenate(
                [state[slot].astype(F32), state[slot + 1].astype(F32)], axis=0))
        low, high = res_ref[0:HALF, cols], res_ref[HALF : 2 * HALF, cols]
        weight = jnp.concatenate([low, low, high, high], axis=0)
        scaled = (jnp.concatenate(pieces, axis=1) * weight).astype(BF16)
        conv = jnp.dot(spread[:, : 2 * modes], scaled, preferred_element_type=F32)
        out_ref[cols, :] = (query_s[:, cols] * (base_s[:, cols] + conv)).T.astype(BF16)

    put = pltpu.make_async_copy(out_ref, out_hbm, local_sem.at[0])
    put.start()
    land(dp_n, over_dp(True))
    total = parts[0].astype(F32)
    for index in range(1, dp_n):
        total = total + parts[index].astype(F32)
    grads[me] = total
    out_e, in_e = over_ctx(lambda peer: grads.at[me], grads, sem_e, rsem_e)
    run(ctx_n, out_e)
    left(ctx_n, out_a)
    left(ctx_n, out_b)
    left(ctx_n, out_f)
    put.wait()
    left(dp_n, over_dp(False))
    land(ctx_n, in_e)
    for half in range(2):
        rate = zero
        for group in range(ctx_n // 2):
            piece = grads[group * 2 + half]
            gres_ref[half * HALF : (half + 1) * HALF, group * LANES : (group + 1) * LANES] = piece[:HALF]
            rate = rate + piece[HALF:]
        rate = jnp.sum(rate, axis=1, keepdims=True) * (2.0 / LANES)
        grate_ref[half * HALF : (half + 1) * HALF, :] = jnp.broadcast_to(rate, (HALF, LANES))
    left(ctx_n, out_e)


def per_device(dp_n, token_ids, feature_table, short_weight, residue, rates, skip_gain, grad_out):
    block = token_ids.shape[1]
    ctx_n = lax.axis_size("ctx")
    channels, modes = residue.shape
    vocab = feature_table.shape[1]
    taps = short_weight.shape[1]

    dma = pltpu.SemaphoreType.DMA
    vmem = pl.BlockSpec(memory_space=pltpu.VMEM)
    hbm = pl.BlockSpec(memory_space=pltpu.HBM)
    previous = pl.pallas_call(
        functools.partial(ids_kernel, ctx_n),
        in_specs=[vmem],
        out_specs=vmem,
        out_shape=jax.ShapeDtypeStruct(token_ids.shape, token_ids.dtype),
        scratch_shapes=[dma, dma],
        compiler_params=pltpu.CompilerParams(collective_id=1, has_side_effects=True),
    )(token_ids)
    mixed, grad_res, grad_rate = pl.pallas_call(
        functools.partial(layer_kernel, ctx_n, dp_n),
        in_specs=[pl.BlockSpec(memory_space=pltpu.SMEM)] + [hbm] * 7,
        out_specs=[hbm, vmem, vmem],
        out_shape=[jax.ShapeDtypeStruct((channels, block), BF16),
                   jax.ShapeDtypeStruct((modes, channels), F32),
                   jax.ShapeDtypeStruct((modes, LANES), F32)],
        scratch_shapes=[
            pltpu.VMEM(token_ids.shape, jnp.int32),
            pltpu.VMEM(token_ids.shape, jnp.int32),
            pltpu.VMEM((taps, 3 * channels), F32),
            pltpu.VMEM((modes, channels), F32),
            pltpu.VMEM((1, channels), F32),
            pltpu.VMEM((channels, block), BF16),
            pltpu.VMEM((block, channels), BF16),
            pltpu.VMEM((block, channels), F32),
            pltpu.VMEM((ctx_n, 16, LANES), BF16),
            pltpu.VMEM((ctx_n, 16, LANES), BF16),
            pltpu.VMEM((3, channels, vocab), BF16),
            pltpu.VMEM((channels, block), BF16),
            pltpu.VMEM((2 * modes * block, block), BF16),
            pltpu.VMEM((4 * modes, block), F32),
            pltpu.VMEM((4 * modes, block), F32),
            pltpu.VMEM((block, block), BF16),
            pltpu.VMEM((modes, LANES), F32),
            pltpu.VMEM((3, block + 8, TILE), F32),
            pltpu.VMEM((2 * modes, TILE), F32),
            pltpu.VMEM((block, channels), F32),
            pltpu.VMEM((block, channels), F32),
            pltpu.VMEM((ctx_n, 64, LANES), F32),
            pltpu.VMEM((ctx_n, 64, LANES), F32),
            pltpu.VMEM((ctx_n, 16, LANES), BF16),
            pltpu.VMEM((ctx_n, 16, LANES), BF16),
            pltpu.VMEM((dp_n, 16, LANES), BF16),
            pltpu.VMEM((ctx_n, 16, LANES), F32),
            dma((ctx_n,)), dma((ctx_n,)), dma((dp_n,)), dma((ctx_n,)), dma((ctx_n,)),
            dma((ctx_n,)), dma((ctx_n,)), dma((dp_n,)), dma((ctx_n,)), dma((ctx_n,)),
            dma((channels // TILE + 6,)),
        ],
        compiler_params=pltpu.CompilerParams(
            collective_id=0, has_side_effects=True, vmem_limit_bytes=67043328),
    )(rates, token_ids, previous, short_weight.T, residue.T, skip_gain[None, :],
      feature_table.reshape(3, channels, vocab), grad_out[0])
    return (mixed[None], grad_res.T, grad_rate[:, 0])


def solution(mesh):
    return jax.shard_map(
        functools.partial(per_device, mesh.shape["dp"]),
        mesh=mesh,
        in_specs=(P("dp", "ctx"), P(), P(), P(), P(), P(), P("dp", None, "ctx")),
        out_specs=(P("dp", None, "ctx"), P(), P()),
        check_vma=False,
    )
```

```python
import functools
import math

import jax
import jax.numpy as jnp
from jax import lax
from jax.experimental import pallas as pl
from jax.experimental.pallas import tpu as pltpu
from jax.sharding import PartitionSpec as P

MESH = pl.DeviceIdType.MESH
F32 = jnp.float32
BF16 = jnp.bfloat16
TILE = 256
HALF = 8
LANES = 128


def layer_kernel(ctx_n, dp_n, rates_ref, ids_hbm, short_hbm, res_hbm, skip_hbm, table_hbm, gout_hbm,
                 out_hbm, grad_ref,
                 ids_ref, prev_ref, short_ref, res_ref, skip_ref, out_ref, gated_s, dconv_s, late, got_late,
                 table, gout, dense, into, onto, spread, rate_rows, feat, sums, query_s, base_s,
                 msg, got, backs, state, parts, grads,
                 sem_a, sem_b, sem_c, sem_e, sem_f, ids_sem, rsem_a, rsem_b, rsem_c, rsem_e, rsem_f, local_sem):
    me = lax.axis_index("ctx")
    rank = lax.axis_index("dp")
    modes, channels = res_ref.shape
    block = out_ref.shape[1]
    vocab = table.shape[2]
    taps = short_ref.shape[0]
    seq_len = block * ctx_n
    tiles = channels // TILE
    period = 2 * modes + 2

    barrier = pltpu.get_barrier_semaphore()

    def greet_dp(step, carry):
        pl.semaphore_signal(barrier, inc=1, device_id={"dp": lax.rem(rank + step, dp_n)}, device_id_type=MESH)
        return carry

    def greet_ctx(step, carry):
        pl.semaphore_signal(barrier, inc=1, device_id={"ctx": lax.rem(me + step, ctx_n)}, device_id_type=MESH)
        return carry

    lax.fori_loop(1, dp_n, greet_dp, 0)
    lax.fori_loop(1, ctx_n, greet_ctx, 0)

    small = []
    pairs = ((ids_hbm, ids_ref), (short_hbm, short_ref), (res_hbm, res_ref),
             (skip_hbm, skip_ref), (gout_hbm, gout))
    for index, (source, target) in enumerate(pairs):
        small.append(pltpu.make_async_copy(source, target, local_sem.at[tiles + index]))
        small[-1].start()
    loads = []
    for tile in range(tiles):
        part = pl.ds(tile * TILE, TILE)
        loads.append(pltpu.make_async_copy(table_hbm.at[:, part], table.at[:, part], local_sem.at[tile]))
        loads[-1].start()

    grad_ref[...] = jnp.zeros_like(grad_ref)

    def wave_angle(product):
        turns = jnp.floor(product * (1.0 / period))
        return (product - period * turns) * (2.0 * math.pi / period)

    for mode in range(modes):
        rate_rows[mode : mode + 1, :] = jnp.full((1, LANES), rates_ref[mode], F32)
    decay_rows = rate_rows[...] * (-1.0 / seq_len)
    number = lax.broadcasted_iota(jnp.int32, (modes, block), 0).astype(F32) + 1.0
    lane = lax.broadcasted_iota(jnp.int32, (modes, block), 1).astype(F32)

    def fill(ref, steps):
        size = jnp.exp(decay_rows * steps)
        angle = wave_angle(number * steps)
        real, imag = size * jnp.cos(angle), size * jnp.sin(angle)
        weight = steps * (1.0 / seq_len)
        for index, value in enumerate((real, imag, real * weight, imag * weight)):
            for half in range(2):
                ref[half * 32 + index * HALF : half * 32 + (index + 1) * HALF, :] = value[half * HALF : (half + 1) * HALF]
        return real, imag

    fill(into, (block - 1.0) - lane)
    real, imag = fill(onto, lane + 1.0)
    spread[...] = jnp.concatenate(
        [real[:HALF], -imag[:HALF], real[HALF:], -imag[HALF:], jnp.zeros((block - 2 * modes, block), F32)],
        axis=0).T.astype(BF16)

    gap = (lax.broadcasted_iota(jnp.int32, (block, block), 0)
           - lax.broadcasted_iota(jnp.int32, (block, block), 1)).astype(F32)
    delay = jnp.where(gap < 0.0, gap + seq_len, gap)
    base_wave = jnp.cos(wave_angle(delay))
    share = delay * (-1.0 / seq_len)

    def fill_dense(mode, carry):
        before, now = carry
        power = jnp.exp(share * rates_ref[mode]) * now
        row = pl.multiple_of(mode * 2 * block, 2 * block)
        dense[pl.ds(row, block), :] = power.astype(BF16)
        dense[pl.ds(row + block, block), :] = (power * share).astype(BF16)
        return now, 2.0 * base_wave * now - before


    for copy in small:
        copy.wait()
    pl.semaphore_wait(barrier, ctx_n - 1 + dp_n - 1)
    pass_ids = pltpu.make_async_remote_copy(
        src_ref=ids_ref, dst_ref=prev_ref, send_sem=ids_sem.at[0], recv_sem=ids_sem.at[1],
        device_id={"ctx": lax.rem(me + 1, ctx_n)}, device_id_type=MESH)
    pass_ids.start()
    lax.fori_loop(0, modes, fill_dense, (jnp.ones((block, block), F32), base_wave))
    pass_ids.wait()

    def spell(ref):
        square = jnp.broadcast_to(ref[...].astype(F32), (block, block)).T
        return jnp.concatenate([square] * (vocab // block), axis=1)

    symbols = jnp.concatenate([spell(prev_ref)[block - 8 :], spell(ids_ref)], axis=0)
    columns = lax.broadcasted_iota(jnp.int32, symbols.shape, 1).astype(F32)
    onehot = jnp.where(columns == symbols, 1.0, 0.0).astype(BF16)

    def halves(value):
        upper = value.astype(BF16)
        return upper, (value - upper.astype(F32)).astype(BF16)

    into_b = jnp.concatenate(halves(into[...]), axis=0)
    onto_b = jnp.concatenate(halves(onto[...]), axis=0)
    states_n = 4 * modes

    for tile in range(tiles):
        loads[tile].wait()
        at = tile * TILE
        cols = pl.ds(at, TILE)
        mixed = []
        for part in range(3):
            feat[part] = lax.dot_general(
                onehot, table[part, cols, :], (((1,), (1,)), ((), ())), preferred_element_type=F32)
            wide = pl.ds(part * channels + at, TILE)
            total = short_ref[0:1, wide] * feat[part, 2 : 2 + block, :]
            for tap in range(1, taps):
                total = total + short_ref[tap : tap + 1, wide] * feat[part, 2 + tap : 2 + tap + block, :]
            mixed.append(total)
        gated = (mixed[1] * mixed[2]).astype(BF16)
        dconv = mixed[0] * gout[cols, :].astype(F32).T
        query_s[:, cols] = mixed[0]
        gated_s[:, cols] = gated
        dconv_s[:, cols] = dconv
        upper = jnp.dot(into_b, gated, preferred_element_type=F32)
        upper = upper[:states_n] + upper[states_n:]
        dconv_u, dconv_l = halves(dconv)
        lower = jnp.dot(onto_b, dconv_u, preferred_element_type=F32)
        lower = lower[:states_n] + lower[states_n:]
        lower = lower + jnp.dot(onto_b[:states_n], dconv_l, preferred_element_type=F32)
        for group in range(TILE // LANES):
            cut = slice(group * LANES, (group + 1) * LANES)
            for half in range(2):
                slot = (TILE // LANES * tile + group) * 2 + half
                msg[slot, 0:32, :] = upper[half * 32 : half * 32 + 32, cut]
                msg[slot, 32:64, :] = lower[half * 32 : half * 32 + 32, cut]

    def run(count, make):
        def body(step, carry):
            make(step).start()
            return carry
        lax.fori_loop(1, count, body, 0)

    def land(count, make):
        def body(step, carry):
            make(step).wait_recv()
            return carry
        lax.fori_loop(1, count, body, 0)

    def left(count, make):
        def body(step, carry):
            make(step).wait_send()
            return carry
        lax.fori_loop(1, count, body, 0)

    def over_ctx(source, target, send, recv):
        def make(step, arriving):
            peer = lax.rem(me + step, ctx_n)
            slot = lax.rem(me + ctx_n - step, ctx_n) if arriving else me
            return pltpu.make_async_remote_copy(
                src_ref=source(peer), dst_ref=target.at[slot], send_sem=send.at[step],
                recv_sem=recv.at[slot], device_id={"ctx": peer}, device_id_type=MESH)
        return (lambda step: make(step, False)), (lambda step: make(step, True))

    out_a, in_a = over_ctx(lambda peer: msg.at[peer], got, sem_a, rsem_a)
    run(ctx_n, out_a)
    own = pltpu.make_async_copy(msg.at[me], got.at[me], local_sem.at[0])
    own.start()

    for tile in range(tiles):
        cols = pl.ds(tile * TILE, TILE)
        gated, dconv = gated_s[:, cols], dconv_s[:, cols]
        base = skip_ref[:, cols] * gated.astype(F32)
        for mode in range(modes):
            row = 2 * mode * block
            both = jnp.dot(dense[row : row + 2 * block, :], gated, preferred_element_type=F32)
            for kind in range(2):
                term = both[kind * block : (kind + 1) * block]
                if kind == 0:
                    base = base + res_ref[mode : mode + 1, cols] * term
                slot = (mode // HALF) * 2 * HALF + kind * HALF + mode % HALF
                sums[slot : slot + 1, :] = jnp.sum(dconv * term, axis=0, keepdims=True)
        base_s[:, cols] = base
        totals = sums[...].astype(BF16)
        for group in range(TILE // LANES):
            cut = slice(group * LANES, (group + 1) * LANES)
            for half in range(2):
                slot = (TILE // LANES * tile + group) * 2 + half
                late[slot] = totals[half * 16 : half * 16 + 16, cut]

    out_f, in_f = over_ctx(lambda peer: late.at[peer], got_late, sem_f, rsem_f)
    run(ctx_n, out_f)
    own_late = pltpu.make_async_copy(late.at[me], got_late.at[me], local_sem.at[2])
    own_late.start()

    own_half = lax.rem(me, 2)
    own_group = me // 2
    first = pl.multiple_of(own_half * HALF, HALF)
    own_decay = rate_rows[pl.ds(first, HALF), :] * (-1.0 / seq_len)
    own_res = res_ref[pl.ds(first, HALF), pl.ds(pl.multiple_of(own_group * LANES, LANES), LANES)]
    own_number = (lax.broadcasted_iota(jnp.int32, (HALF, LANES), 0) + (own_half * HALF + 1)).astype(F32)

    def turn(steps):
        size = jnp.exp(own_decay * steps)
        angle = wave_angle(own_number * steps)
        return size * jnp.cos(angle), size * jnp.sin(angle)

    turn_c, turn_s = turn(float(block))
    last_c, last_s = turn(float(block * (ctx_n - 2)))
    step_len = 1.0 / ctx_n
    span = step_len * (ctx_n - 2)
    zero = jnp.zeros((HALF, LANES), F32)

    def states(index, start):
        pair = got[index, start : start + 16, :]
        return pair[:HALF], pair[HALF:]

    def times_turn(real, imag):
        return real * turn_c - imag * turn_s, real * turn_s + imag * turn_c

    def times_last(real, imag):
        return real * last_c - imag * last_s, real * last_s + imag * last_c

    def advance(index, carry):
        hr, hi, dr, di = carry
        ur, ui = states(index, 0)
        wr, wi = states(index, 16)
        nr, ni = times_turn(hr, hi)
        er, ei = times_turn(dr + step_len * hr, di + step_len * hi)
        return nr + ur, ni + ui, er + wr, ei + wi

    own.wait()
    land(ctx_n, in_a)
    carry = (zero, zero, zero, zero)
    for index in range(1, ctx_n):
        carry = advance(index, carry)
    gsum, dsum = zero, zero
    for index in range(ctx_n):
        hr, hi, dr, di = carry
        backs[index] = jnp.concatenate([hr, hi], axis=0).astype(BF16)
        vr, vi = states(index, 32)
        xr, xi = states(index, 48)
        gsum = gsum + (vr * hr - vi * hi)
        dsum = dsum - ((xr * hr - xi * hi) + (vr * dr - vi * di))
        if index < ctx_n - 1:
            ur, ui = states(index + 1, 0)
            wr, wi = states(index + 1, 16)
            lr, li = times_last(ur, ui)
            pr, pi_ = times_last(wr + span * ur, wi + span * ui)
            carry = advance(index, (hr - lr, hi - li, dr - pr, di - pi_))

    out_b, in_b = over_ctx(lambda peer: backs.at[peer], state, sem_b, rsem_b)
    run(ctx_n, out_b)
    mine = pltpu.make_async_copy(backs.at[me], state.at[me], local_sem.at[1])
    mine.start()
    own_late.wait()
    land(ctx_n, in_f)
    for index in range(ctx_n):
        pair = got_late[index].astype(F32)
        gsum = gsum + pair[:HALF]
        dsum = dsum + pair[HALF:]
    rate = jnp.broadcast_to(jnp.sum(dsum * own_res, axis=1, keepdims=True), (HALF, LANES))
    rate_u, rate_l = halves(rate)
    left_half = lax.broadcasted_iota(jnp.int32, (HALF, LANES), 1) < LANES // 2
    rate = jnp.where(left_half, rate_u.astype(F32), rate_l.astype(F32))
    parts[rank] = jnp.concatenate([gsum, rate], axis=0).astype(BF16)

    def over_dp(arriving):
        def make(step):
            peer = lax.rem(rank + step, dp_n)
            slot = lax.rem(rank + dp_n - step, dp_n) if arriving else rank
            return pltpu.make_async_remote_copy(
                src_ref=parts.at[rank], dst_ref=parts.at[slot], send_sem=sem_c.at[step],
                recv_sem=rsem_c.at[slot], device_id={"dp": peer}, device_id_type=MESH)
        return make

    run(dp_n, over_dp(False))
    mine.wait()
    land(ctx_n, in_b)

    for tile in range(tiles):
        cols = pl.ds(tile * TILE, TILE)
        pieces = []
        for group in range(TILE // LANES):
            slot = (TILE // LANES * tile + group) * 2
            pieces.append(jnp.concatenate(
                [state[slot].astype(F32), state[slot + 1].astype(F32)], axis=0))
        low, high = res_ref[0:HALF, cols], res_ref[HALF : 2 * HALF, cols]
        weight = jnp.concatenate([low, low, high, high], axis=0)
        scaled = (jnp.concatenate(pieces, axis=1) * weight).astype(BF16)
        conv = jnp.dot(spread[:, : 2 * modes], scaled, preferred_element_type=F32)
        out_ref[cols, :] = (query_s[:, cols] * (base_s[:, cols] + conv)).T.astype(BF16)

    put = pltpu.make_async_copy(out_ref, out_hbm, local_sem.at[0])
    put.start()
    land(dp_n, over_dp(True))
    total = parts[0].astype(F32)
    for index in range(1, dp_n):
        total = total + parts[index].astype(F32)
    grads[me] = total
    out_e, in_e = over_ctx(lambda peer: grads.at[me], grads, sem_e, rsem_e)
    run(ctx_n, out_e)
    left(ctx_n, out_a)
    left(ctx_n, out_b)
    left(ctx_n, out_f)
    line = jnp.zeros((1, LANES), F32)
    put.wait()
    left(dp_n, over_dp(False))
    land(ctx_n, in_e)
    for half in range(2):
        rate = zero
        for group in range(ctx_n // 2):
            piece = grads[group * 2 + half]
            grad_ref[half * HALF : (half + 1) * HALF, group * LANES : (group + 1) * LANES] = piece[:HALF]
            rate = rate + piece[HALF:]
        rate = jnp.sum(rate, axis=1, keepdims=True) * (2.0 / LANES)
        spot = lax.broadcasted_iota(jnp.int32, (HALF, LANES), 1)
        spot = spot == lax.broadcasted_iota(jnp.int32, (HALF, LANES), 0) + half * HALF
        line = line + jnp.sum(jnp.where(spot, rate, 0.0), axis=0, keepdims=True)
    grad_ref[modes : modes + 1, 0:LANES] = line
    left(ctx_n, out_e)


def per_device(dp_n, token_ids, feature_table, short_weight, residue, rates, skip_gain, grad_out):
    block = token_ids.shape[1]
    ctx_n = lax.axis_size("ctx")
    channels, modes = residue.shape
    vocab = feature_table.shape[1]
    taps = short_weight.shape[1]

    dma = pltpu.SemaphoreType.DMA
    vmem = pl.BlockSpec(memory_space=pltpu.VMEM)
    hbm = pl.BlockSpec(memory_space=pltpu.HBM)
    mixed, grads = pl.pallas_call(
        functools.partial(layer_kernel, ctx_n, dp_n),
        in_specs=[pl.BlockSpec(memory_space=pltpu.SMEM)] + [hbm] * 6,
        out_specs=[hbm, vmem],
        out_shape=[jax.ShapeDtypeStruct((channels, block), BF16),
                   jax.ShapeDtypeStruct((modes + 8, channels), F32)],
        scratch_shapes=[
            pltpu.VMEM(token_ids.shape, jnp.int32),
            pltpu.VMEM(token_ids.shape, jnp.int32),
            pltpu.VMEM((taps, 3 * channels), F32),
            pltpu.VMEM((modes, channels), F32),
            pltpu.VMEM((1, channels), F32),
            pltpu.VMEM((channels, block), BF16),
            pltpu.VMEM((block, channels), BF16),
            pltpu.VMEM((block, channels), F32),
            pltpu.VMEM((ctx_n, 16, LANES), BF16),
            pltpu.VMEM((ctx_n, 16, LANES), BF16),
            pltpu.VMEM((3, channels, vocab), BF16),
            pltpu.VMEM((channels, block), BF16),
            pltpu.VMEM((2 * modes * block, block), BF16),
            pltpu.VMEM((4 * modes, block), F32),
            pltpu.VMEM((4 * modes, block), F32),
            pltpu.VMEM((block, block), BF16),
            pltpu.VMEM((modes, LANES), F32),
            pltpu.VMEM((3, block + 8, TILE), F32),
            pltpu.VMEM((2 * modes, TILE), F32),
            pltpu.VMEM((block, channels), F32),
            pltpu.VMEM((block, channels), F32),
            pltpu.VMEM((ctx_n, 64, LANES), F32),
            pltpu.VMEM((ctx_n, 64, LANES), F32),
            pltpu.VMEM((ctx_n, 16, LANES), BF16),
            pltpu.VMEM((ctx_n, 16, LANES), BF16),
            pltpu.VMEM((dp_n, 16, LANES), BF16),
            pltpu.VMEM((ctx_n, 16, LANES), F32),
            dma((ctx_n,)), dma((ctx_n,)), dma((dp_n,)), dma((ctx_n,)), dma((ctx_n,)), dma((2,)),
            dma((ctx_n,)), dma((ctx_n,)), dma((dp_n,)), dma((ctx_n,)), dma((ctx_n,)),
            dma((channels // TILE + 5,)),
        ],
        compiler_params=pltpu.CompilerParams(
            collective_id=0, has_side_effects=True, vmem_limit_bytes=67043328),
    )(rates, token_ids, short_weight.T, residue.T, skip_gain[None, :],
      feature_table.reshape(3, channels, vocab), grad_out[0])
    return (mixed[None], grads[:modes].T, grads[modes, :modes])


def solution(mesh):
    return jax.shard_map(
        functools.partial(per_device, mesh.shape["dp"]),
        mesh=mesh,
        in_specs=(P("dp", "ctx"), P(), P(), P(), P(), P(), P("dp", None, "ctx")),
        out_specs=(P("dp", None, "ctx"), P(), P()),
        check_vma=False,
    )
```

```python
import functools
import math

import jax
import jax.numpy as jnp
from jax import lax
from jax.experimental import pallas as pl
from jax.experimental.pallas import tpu as pltpu
from jax.sharding import PartitionSpec as P

MESH = pl.DeviceIdType.MESH
F32 = jnp.float32
BF16 = jnp.bfloat16
TILE = 256
HALF = 8
LANES = 128


def layer_kernel(ctx_n, dp_n, rates_ref, ids_hbm, short_hbm, res_hbm, skip_hbm, table_hbm, gout_hbm,
                 out_hbm, grad_ref,
                 ids_ref, prev_ref, short_ref, res_ref, skip_ref, out_ref, gated_s, dconv_s, late, got_late,
                 table, gout, dense, into, onto, spread, rate_rows, feat, sums, query_s, base_s,
                 msg, got, backs, state, parts, grads,
                 sem_a, sem_b, sem_c, sem_e, sem_f, ids_sem, rsem_a, rsem_b, rsem_c, rsem_e, rsem_f, local_sem):
    me = lax.axis_index("ctx")
    rank = lax.axis_index("dp")
    modes, channels = res_ref.shape
    block = out_ref.shape[1]
    vocab = table.shape[2]
    taps = short_ref.shape[0]
    seq_len = block * ctx_n
    tiles = channels // TILE
    period = 2 * modes + 2

    barrier = pltpu.get_barrier_semaphore()

    def greet_dp(step, carry):
        pl.semaphore_signal(barrier, inc=1, device_id={"dp": lax.rem(rank + step, dp_n)}, device_id_type=MESH)
        return carry

    def greet_ctx(step, carry):
        pl.semaphore_signal(barrier, inc=1, device_id={"ctx": lax.rem(me + step, ctx_n)}, device_id_type=MESH)
        return carry

    lax.fori_loop(1, dp_n, greet_dp, 0)
    lax.fori_loop(1, ctx_n, greet_ctx, 0)

    small = []
    pairs = ((ids_hbm, ids_ref), (short_hbm, short_ref), (res_hbm, res_ref),
             (skip_hbm, skip_ref), (gout_hbm, gout))
    for index, (source, target) in enumerate(pairs):
        small.append(pltpu.make_async_copy(source, target, local_sem.at[tiles + index]))
        small[-1].start()
    loads = []
    owners = 2 * TILE // LANES

    def spin(index):
        return lax.rem(me // owners + index, tiles)

    for tile in range(tiles):
        part = pl.ds(pl.multiple_of(spin(tile) * TILE, TILE), TILE)
        loads.append(pltpu.make_async_copy(table_hbm.at[:, part], table.at[:, part], local_sem.at[tile]))
        loads[-1].start()

    grad_ref[...] = jnp.zeros_like(grad_ref)

    def wave_angle(product):
        turns = jnp.floor(product * (1.0 / period))
        return (product - period * turns) * (2.0 * math.pi / period)

    for mode in range(modes):
        rate_rows[mode : mode + 1, :] = jnp.full((1, LANES), rates_ref[mode], F32)
    decay_rows = rate_rows[...] * (-1.0 / seq_len)
    number = lax.broadcasted_iota(jnp.int32, (modes, block), 0).astype(F32) + 1.0
    lane = lax.broadcasted_iota(jnp.int32, (modes, block), 1).astype(F32)

    def fill(ref, steps):
        size = jnp.exp(decay_rows * steps)
        angle = wave_angle(number * steps)
        real, imag = size * jnp.cos(angle), size * jnp.sin(angle)
        weight = steps * (1.0 / seq_len)
        for index, value in enumerate((real, imag, real * weight, imag * weight)):
            for half in range(2):
                ref[half * 32 + index * HALF : half * 32 + (index + 1) * HALF, :] = value[half * HALF : (half + 1) * HALF]
        return real, imag

    fill(into, (block - 1.0) - lane)
    real, imag = fill(onto, lane + 1.0)
    spread[...] = jnp.concatenate(
        [real[:HALF], -imag[:HALF], real[HALF:], -imag[HALF:], jnp.zeros((block - 2 * modes, block), F32)],
        axis=0).T.astype(BF16)

    gap = (lax.broadcasted_iota(jnp.int32, (block, block), 0)
           - lax.broadcasted_iota(jnp.int32, (block, block), 1)).astype(F32)
    delay = jnp.where(gap < 0.0, gap + seq_len, gap)
    base_wave = jnp.cos(wave_angle(delay))
    share = delay * (-1.0 / seq_len)

    def fill_dense(mode, carry):
        before, now = carry
        power = jnp.exp(share * rates_ref[mode]) * now
        row = pl.multiple_of(mode * 2 * block, 2 * block)
        dense[pl.ds(row, block), :] = power.astype(BF16)
        dense[pl.ds(row + block, block), :] = (power * share).astype(BF16)
        return now, 2.0 * base_wave * now - before


    for copy in small:
        copy.wait()
    pl.semaphore_wait(barrier, ctx_n - 1 + dp_n - 1)
    pass_ids = pltpu.make_async_remote_copy(
        src_ref=ids_ref, dst_ref=prev_ref, send_sem=ids_sem.at[0], recv_sem=ids_sem.at[1],
        device_id={"ctx": lax.rem(me + 1, ctx_n)}, device_id_type=MESH)
    pass_ids.start()
    lax.fori_loop(0, modes, fill_dense, (jnp.ones((block, block), F32), base_wave))
    pass_ids.wait()

    def spell(ref):
        square = jnp.broadcast_to(ref[...].astype(F32), (block, block)).T
        return jnp.concatenate([square] * (vocab // block), axis=1)

    symbols = jnp.concatenate([spell(prev_ref)[block - 8 :], spell(ids_ref)], axis=0)
    columns = lax.broadcasted_iota(jnp.int32, symbols.shape, 1).astype(F32)
    onehot = jnp.where(columns == symbols, 1.0, 0.0).astype(BF16)

    def halves(value):
        upper = value.astype(BF16)
        return upper, (value - upper.astype(F32)).astype(BF16)

    into_b = jnp.concatenate(halves(into[...]), axis=0)
    onto_b = jnp.concatenate(halves(onto[...]), axis=0)
    states_n = 4 * modes

    def run(count, make):
        def body(step, carry):
            make(step).start()
            return carry
        lax.fori_loop(1, count, body, 0)

    def land(count, make):
        def body(step, carry):
            make(step).wait_recv()
            return carry
        lax.fori_loop(1, count, body, 0)

    def left(count, make):
        def body(step, carry):
            make(step).wait_send()
            return carry
        lax.fori_loop(1, count, body, 0)

    def over_ctx(source, target, send, recv):
        def make(step, arriving):
            peer = lax.rem(me + step, ctx_n)
            slot = lax.rem(me + ctx_n - step, ctx_n) if arriving else me
            return pltpu.make_async_remote_copy(
                src_ref=source(peer), dst_ref=target.at[slot], send_sem=send.at[step],
                recv_sem=recv.at[slot], device_id={"ctx": peer}, device_id_type=MESH)
        return (lambda step: make(step, False)), (lambda step: make(step, True))

    out_a, in_a = over_ctx(lambda peer: msg.at[peer], got, sem_a, rsem_a)

    for turn_at in range(tiles):
        loads[turn_at].wait()
        tile = spin(turn_at)
        at = pl.multiple_of(tile * TILE, TILE)
        cols = pl.ds(at, TILE)
        mixed = []
        for part in range(3):
            feat[part] = lax.dot_general(
                onehot, table[part, cols, :], (((1,), (1,)), ((), ())), preferred_element_type=F32)
            wide = pl.ds(pl.multiple_of(part * channels + at, TILE), TILE)
            total = short_ref[0:1, wide] * feat[part, 2 : 2 + block, :]
            for tap in range(1, taps):
                total = total + short_ref[tap : tap + 1, wide] * feat[part, 2 + tap : 2 + tap + block, :]
            mixed.append(total)
        gated = (mixed[1] * mixed[2]).astype(BF16)
        dconv = mixed[0] * gout[cols, :].astype(F32).T
        query_s[:, cols] = mixed[0]
        gated_s[:, cols] = gated
        dconv_s[:, cols] = dconv
        upper = jnp.dot(into_b, gated, preferred_element_type=F32)
        upper = upper[:states_n] + upper[states_n:]
        dconv_u, dconv_l = halves(dconv)
        lower = jnp.dot(onto_b, dconv_u, preferred_element_type=F32)
        lower = lower[:states_n] + lower[states_n:]
        lower = lower + jnp.dot(onto_b[:states_n], dconv_l, preferred_element_type=F32)
        for group in range(TILE // LANES):
            cut = slice(group * LANES, (group + 1) * LANES)
            for half in range(2):
                slot = (TILE // LANES * tile + group) * 2 + half
                msg[slot, 0:32, :] = upper[half * 32 : half * 32 + 32, cut]
                msg[slot, 32:64, :] = lower[half * 32 : half * 32 + 32, cut]
        for index in range(owners):
            away = lax.rem(tile * owners + lax.rem(index + me, owners) + ctx_n - me, ctx_n)

            @pl.when(away != 0)
            def _():
                out_a(away).start()

    own = pltpu.make_async_copy(msg.at[me], got.at[me], local_sem.at[0])
    own.start()

    for tile in range(tiles):
        cols = pl.ds(tile * TILE, TILE)
        gated, dconv = gated_s[:, cols], dconv_s[:, cols]
        base = skip_ref[:, cols] * gated.astype(F32)
        for mode in range(modes):
            row = 2 * mode * block
            both = jnp.dot(dense[row : row + 2 * block, :], gated, preferred_element_type=F32)
            for kind in range(2):
                term = both[kind * block : (kind + 1) * block]
                if kind == 0:
                    base = base + res_ref[mode : mode + 1, cols] * term
                slot = (mode // HALF) * 2 * HALF + kind * HALF + mode % HALF
                sums[slot : slot + 1, :] = jnp.sum(dconv * term, axis=0, keepdims=True)
        base_s[:, cols] = base
        totals = sums[...].astype(BF16)
        for group in range(TILE // LANES):
            cut = slice(group * LANES, (group + 1) * LANES)
            for half in range(2):
                slot = (TILE // LANES * tile + group) * 2 + half
                late[slot] = totals[half * 16 : half * 16 + 16, cut]

    out_f, in_f = over_ctx(lambda peer: late.at[peer], got_late, sem_f, rsem_f)
    run(ctx_n, out_f)
    own_late = pltpu.make_async_copy(late.at[me], got_late.at[me], local_sem.at[2])
    own_late.start()

    own_half = lax.rem(me, 2)
    own_group = me // 2
    first = pl.multiple_of(own_half * HALF, HALF)
    own_decay = rate_rows[pl.ds(first, HALF), :] * (-1.0 / seq_len)
    own_res = res_ref[pl.ds(first, HALF), pl.ds(pl.multiple_of(own_group * LANES, LANES), LANES)]
    own_number = (lax.broadcasted_iota(jnp.int32, (HALF, LANES), 0) + (own_half * HALF + 1)).astype(F32)

    def turn(steps):
        size = jnp.exp(own_decay * steps)
        angle = wave_angle(own_number * steps)
        return size * jnp.cos(angle), size * jnp.sin(angle)

    turn_c, turn_s = turn(float(block))
    last_c, last_s = turn(float(block * (ctx_n - 2)))
    step_len = 1.0 / ctx_n
    span = step_len * (ctx_n - 2)
    zero = jnp.zeros((HALF, LANES), F32)

    def states(index, start):
        pair = got[index, start : start + 16, :]
        return pair[:HALF], pair[HALF:]

    def times_turn(real, imag):
        return real * turn_c - imag * turn_s, real * turn_s + imag * turn_c

    def times_last(real, imag):
        return real * last_c - imag * last_s, real * last_s + imag * last_c

    def advance(index, carry):
        hr, hi, dr, di = carry
        ur, ui = states(index, 0)
        wr, wi = states(index, 16)
        nr, ni = times_turn(hr, hi)
        er, ei = times_turn(dr + step_len * hr, di + step_len * hi)
        return nr + ur, ni + ui, er + wr, ei + wi

    own.wait()
    land(ctx_n, in_a)
    carry = (zero, zero, zero, zero)
    for index in range(1, ctx_n):
        carry = advance(index, carry)
    gsum, dsum = zero, zero
    for index in range(ctx_n):
        hr, hi, dr, di = carry
        backs[index] = jnp.concatenate([hr, hi], axis=0).astype(BF16)
        vr, vi = states(index, 32)
        xr, xi = states(index, 48)
        gsum = gsum + (vr * hr - vi * hi)
        dsum = dsum - ((xr * hr - xi * hi) + (vr * dr - vi * di))
        if index < ctx_n - 1:
            ur, ui = states(index + 1, 0)
            wr, wi = states(index + 1, 16)
            lr, li = times_last(ur, ui)
            pr, pi_ = times_last(wr + span * ur, wi + span * ui)
            carry = advance(index, (hr - lr, hi - li, dr - pr, di - pi_))

    out_b, in_b = over_ctx(lambda peer: backs.at[peer], state, sem_b, rsem_b)
    run(ctx_n, out_b)
    mine = pltpu.make_async_copy(backs.at[me], state.at[me], local_sem.at[1])
    mine.start()
    own_late.wait()
    land(ctx_n, in_f)
    for index in range(ctx_n):
        pair = got_late[index].astype(F32)
        gsum = gsum + pair[:HALF]
        dsum = dsum + pair[HALF:]
    rate = jnp.broadcast_to(jnp.sum(dsum * own_res, axis=1, keepdims=True), (HALF, LANES))
    rate_u, rate_l = halves(rate)
    left_half = lax.broadcasted_iota(jnp.int32, (HALF, LANES), 1) < LANES // 2
    rate = jnp.where(left_half, rate_u.astype(F32), rate_l.astype(F32))
    parts[rank] = jnp.concatenate([gsum, rate], axis=0).astype(BF16)

    def over_dp(arriving):
        def make(step):
            peer = lax.rem(rank + step, dp_n)
            slot = lax.rem(rank + dp_n - step, dp_n) if arriving else rank
            return pltpu.make_async_remote_copy(
                src_ref=parts.at[rank], dst_ref=parts.at[slot], send_sem=sem_c.at[step],
                recv_sem=rsem_c.at[slot], device_id={"dp": peer}, device_id_type=MESH)
        return make

    run(dp_n, over_dp(False))
    mine.wait()
    land(ctx_n, in_b)

    for tile in range(tiles):
        cols = pl.ds(tile * TILE, TILE)
        pieces = []
        for group in range(TILE // LANES):
            slot = (TILE // LANES * tile + group) * 2
            pieces.append(jnp.concatenate(
                [state[slot].astype(F32), state[slot + 1].astype(F32)], axis=0))
        low, high = res_ref[0:HALF, cols], res_ref[HALF : 2 * HALF, cols]
        weight = jnp.concatenate([low, low, high, high], axis=0)
        scaled = (jnp.concatenate(pieces, axis=1) * weight).astype(BF16)
        conv = jnp.dot(spread[:, : 2 * modes], scaled, preferred_element_type=F32)
        out_ref[cols, :] = (query_s[:, cols] * (base_s[:, cols] + conv)).T.astype(BF16)

    put = pltpu.make_async_copy(out_ref, out_hbm, local_sem.at[0])
    put.start()
    land(dp_n, over_dp(True))
    total = parts[0].astype(F32)
    for index in range(1, dp_n):
        total = total + parts[index].astype(F32)
    grads[me] = total
    out_e, in_e = over_ctx(lambda peer: grads.at[me], grads, sem_e, rsem_e)
    run(ctx_n, out_e)
    left(ctx_n, out_a)
    left(ctx_n, out_b)
    left(ctx_n, out_f)
    line = jnp.zeros((1, LANES), F32)
    put.wait()
    left(dp_n, over_dp(False))
    land(ctx_n, in_e)
    for half in range(2):
        rate = zero
        for group in range(ctx_n // 2):
            piece = grads[group * 2 + half]
            grad_ref[half * HALF : (half + 1) * HALF, group * LANES : (group + 1) * LANES] = piece[:HALF]
            rate = rate + piece[HALF:]
        rate = jnp.sum(rate, axis=1, keepdims=True) * (2.0 / LANES)
        spot = lax.broadcasted_iota(jnp.int32, (HALF, LANES), 1)
        spot = spot == lax.broadcasted_iota(jnp.int32, (HALF, LANES), 0) + half * HALF
        line = line + jnp.sum(jnp.where(spot, rate, 0.0), axis=0, keepdims=True)
    grad_ref[modes : modes + 1, 0:LANES] = line
    left(ctx_n, out_e)


def per_device(dp_n, token_ids, feature_table, short_weight, residue, rates, skip_gain, grad_out):
    block = token_ids.shape[1]
    ctx_n = lax.axis_size("ctx")
    channels, modes = residue.shape
    vocab = feature_table.shape[1]
    taps = short_weight.shape[1]

    dma = pltpu.SemaphoreType.DMA
    vmem = pl.BlockSpec(memory_space=pltpu.VMEM)
    hbm = pl.BlockSpec(memory_space=pltpu.HBM)
    mixed, grads = pl.pallas_call(
        functools.partial(layer_kernel, ctx_n, dp_n),
        in_specs=[pl.BlockSpec(memory_space=pltpu.SMEM)] + [hbm] * 6,
        out_specs=[hbm, vmem],
        out_shape=[jax.ShapeDtypeStruct((channels, block), BF16),
                   jax.ShapeDtypeStruct((modes + 8, channels), F32)],
        scratch_shapes=[
            pltpu.VMEM(token_ids.shape, jnp.int32),
            pltpu.VMEM(token_ids.shape, jnp.int32),
            pltpu.VMEM((taps, 3 * channels), F32),
            pltpu.VMEM((modes, channels), F32),
            pltpu.VMEM((1, channels), F32),
            pltpu.VMEM((channels, block), BF16),
            pltpu.VMEM((block, channels), BF16),
            pltpu.VMEM((block, channels), F32),
            pltpu.VMEM((ctx_n, 16, LANES), BF16),
            pltpu.VMEM((ctx_n, 16, LANES), BF16),
            pltpu.VMEM((3, channels, vocab), BF16),
            pltpu.VMEM((channels, block), BF16),
            pltpu.VMEM((2 * modes * block, block), BF16),
            pltpu.VMEM((4 * modes, block), F32),
            pltpu.VMEM((4 * modes, block), F32),
            pltpu.VMEM((block, block), BF16),
            pltpu.VMEM((modes, LANES), F32),
            pltpu.VMEM((3, block + 8, TILE), F32),
            pltpu.VMEM((2 * modes, TILE), F32),
            pltpu.VMEM((block, channels), F32),
            pltpu.VMEM((block, channels), F32),
            pltpu.VMEM((ctx_n, 64, LANES), F32),
            pltpu.VMEM((ctx_n, 64, LANES), F32),
            pltpu.VMEM((ctx_n, 16, LANES), BF16),
            pltpu.VMEM((ctx_n, 16, LANES), BF16),
            pltpu.VMEM((dp_n, 16, LANES), BF16),
            pltpu.VMEM((ctx_n, 16, LANES), F32),
            dma((ctx_n,)), dma((ctx_n,)), dma((dp_n,)), dma((ctx_n,)), dma((ctx_n,)), dma((2,)),
            dma((ctx_n,)), dma((ctx_n,)), dma((dp_n,)), dma((ctx_n,)), dma((ctx_n,)),
            dma((channels // TILE + 5,)),
        ],
        compiler_params=pltpu.CompilerParams(
            collective_id=0, has_side_effects=True, vmem_limit_bytes=67043328),
    )(rates, token_ids, short_weight.T, residue.T, skip_gain[None, :],
      feature_table.reshape(3, channels, vocab), grad_out[0])
    return (mixed[None], grads[:modes].T, grads[modes, :modes])


def solution(mesh):
    return jax.shard_map(
        functools.partial(per_device, mesh.shape["dp"]),
        mesh=mesh,
        in_specs=(P("dp", "ctx"), P(), P(), P(), P(), P(), P("dp", None, "ctx")),
        out_specs=(P("dp", None, "ctx"), P(), P()),
        check_vma=False,
    )
```
